512 devices in a mesh: bin: 64 (over z, y), wave: 8 (over x, core).
Axes of the slice: x: 4, y: 8, z: 8, core: 2. Of those that a mesh axis runs over, the one named last changes fastest.
Arguments:
- sources: bfloat16 [262144, 256], P(('bin', 'wave')), may hold values from -6 to 6
- density: bfloat16 [262144], P(('bin', 'wave')), may hold values from 0.5 to 1.5
- temp_bins: int32 [262144, 1], P(('bin', 'wave')), may hold values from 0 to 63; in each aligned block of 512 rows (0 to 511, 512 to 1023, ...) at most 16 rows name the same one
- ray_index: int32 [262144], P(('bin', 'wave')), may hold values from 0 to 1023
- rate_tables: bfloat16 [64, 256, 256], P('bin'), as said below
- line_table: bfloat16 [256, 8192], P(None, 'wave'), may hold values from -0.0234375 to 0.0234375
Outputs:
- intensity: float32 [1024, 8192], P('bin', 'wave')
The draws below stay inside these ranges and needn't reach their ends.
Inputs may be any that keep to these rules, and one draw needn't show every extreme that they name: `temp_bins`: among the 512 cells of one device (aligned blocks of 512 rows) no bin is named more than 16 times; some bin is named exactly 16 times. `rate_tables`: each bin's matrix has a diagonal between 0.25 and 0.55 and independent off-diagonal entries.
All inputs are finite; a program needn't handle non-finite values.
Results may differ from the reference program's by a relative error of at most 0.005.
Values may be sent and summed in bfloat16 or wider, within the bound.
A program may use at most 64 MiB of HBM per device.

```python
import math
import jax
import jax.numpy as jnp
import numpy as np
from jax import lax

L = 256
W = 8192
C = 512
BINS = 64
CAP = 16
CELLS = 262144
RAYS = 1024
N_BIN = 64
N_WAVE = 8


def draw_rate_tables(key, part):
    key_diag = jax.random.fold_in(key, 11)
    key_off = jax.random.fold_in(key, 23)
    diag_values = jax.random.uniform(key_diag, (BINS, L), jnp.float32, 0.3, 0.5)
    off_values = jax.random.normal(key_off, (BINS, L, L), jnp.float32) * (0.3 / jnp.sqrt(1.0 * L))
    eye_mask = (jnp.arange(L)[:, None] == jnp.arange(L)[None, :]).astype(jnp.float32)
    tables = off_values * (1.0 - eye_mask)[None, :, :] + eye_mask[None, :, :] * diag_values[:, None, :]
    return tables.astype(jnp.bfloat16)


def set_ends(result, stream_key, smallest, largest):
    longest = result.shape.index(max(result.shape))
    spots = []
    for shift in (0, 1):
        where = [jax.random.randint(jax.random.fold_in(stream_key, axis), (), 0, length) for axis, length in enumerate(result.shape)]
        where[longest] = (where[longest] + shift) % result.shape[longest]
        spots.append(tuple(where))
    return result.at[spots[0]].set(smallest).at[spots[1]].set(largest)


def levels(stream_key, extent, cuts, smallest, top_value):
    def one(axis_at, parts):
        heights = jax.random.uniform(jax.random.fold_in(jax.random.fold_in(stream_key, 6), axis_at), (parts,), jnp.float32, smallest / len(cuts), top_value / len(cuts))
        return jnp.repeat(jnp.exp(heights), extent[axis_at] // parts).reshape((-1,) + (1,) * (len(extent) - axis_at - 1))

    level = one(*cuts[0])
    for cut in cuts[1:]:
        level = level * one(*cut)
    return level


def routed_block(stream_key, own, number, rows, number_of, top, bound, lean):
    sequence = jax.random.permutation(stream_key, number_of)
    packed, ordinary = shares(number_of, rows * top, bound, lean, True), shares(number_of, rows * top, bound, lean, False)
    places = jnp.arange(number_of)

    def named(lengths, offset_by):
        used = int((lengths > 0).sum())
        fixed = max(1, used // 4)
        shifted = fixed + (places - fixed + offset_by * (used - fixed)) % max(1, number_of - fixed)
        return jnp.zeros((number_of,), jnp.int32).at[sequence[jnp.where(places < fixed, places, shifted)]].set(jnp.asarray(lengths, jnp.int32))

    lengths = jnp.where(number % 4 == 0, named(packed, number // 4), named(ordinary, number - number // 4 - 1))
    mixed = jax.random.permutation(jax.random.fold_in(own, 3), number_of)
    giver, taker = mixed[0:number_of // 2 * 2:2], mixed[1:number_of // 2 * 2:2]
    room = jnp.minimum(lengths[giver] - 1, bound - lengths[taker]) // 2
    room = jnp.where((giver == sequence[0]) | (taker == sequence[0]) | (lengths[taker] == 0), 0, jnp.maximum(room, 0))
    shifted = jax.random.randint(jax.random.fold_in(own, 4), (number_of // 2,), 0, 1 << 20) % (room + 1)
    lengths = lengths.at[giver].add(-shifted).at[taker].add(shifted)
    labels = jnp.searchsorted(jnp.cumsum(lengths), jnp.arange(rows * top), side="right").astype(jnp.int32)
    table = labels.reshape(top, rows).T
    table = table[jax.random.permutation(jax.random.fold_in(own, 1), rows)]
    offset_by = jax.random.randint(jax.random.fold_in(own, 2), (rows, 1), 0, top)
    return jnp.take_along_axis(table, (jnp.arange(top)[None, :] + offset_by) % top, axis=1)


def shares(amount, total, most, slope, full):
    portions = [(1 << 20) // math.isqrt(standing ** slope) + 1 for standing in range(1, amount + 1)]
    largest = most if full else min(most, max(-(-total // amount), total * portions[0] // sum(portions)))
    least = 1 if total - largest >= amount - 1 else 0
    holding, rest = [largest] + [least] * (amount - 1), total - largest - least * (amount - 1)
    while rest > 0:
        free = [i for i in range(1, amount) if holding[i] < largest] or [i for i in range(1, amount) if holding[i] < most]
        mass, left = sum([portions[i] for i in free]), rest
        for i in free:
            addition = min(most - holding[i], max(1, left * portions[i] // mass), rest)
            holding[i] = holding[i] + addition
            rest = rest - addition
    return np.array(holding)


def noise(own_key, dims, scale, bound, cuts=(), held_as=jnp.bfloat16):
    values = jax.random.normal(own_key, dims, jnp.float32) * scale
    if len(cuts) > 0:
        values = levels(own_key, dims, cuts, -0.22, 0.18) * values
    return jnp.clip(values, min=-bound, max=bound).astype(held_as)


def setup_inputs(seed: int = 0) -> dict:
    key_of = jax.random.split(jax.random.key(seed), 7)
    sources = noise(key_of[0], (CELLS, L), 1.0, 6.0, ((0, 512),))
    density = jnp.clip(jnp.exp(math.log(1.5) - 1.0986123 * jax.random.uniform(key_of[1], (CELLS,), jnp.float32) ** levels(key_of[1], (CELLS,), ((0, 512),), -0.2, 0.2)), 0.5, 1.5).astype(jnp.bfloat16)
    temp_bins_keys = jax.random.split(jax.random.fold_in(key_of[2], 1), CELLS // C)
    temp_bins_turns = jax.random.permutation(jax.random.fold_in(key_of[2], 3), CELLS // C)
    temp_bins = jax.vmap(lambda own, number: routed_block(jax.random.fold_in(key_of[2], 2), own, number, C, BINS, 1, CAP, 2))(temp_bins_keys, temp_bins_turns).reshape((CELLS, 1))
    ray_index = set_ends(jax.random.randint(key_of[3], (CELLS,), 0, RAYS), jax.random.fold_in(key_of[3], 1), 0, RAYS - 1).astype(jnp.int32)
    rate_tables = draw_rate_tables(jax.random.fold_in(key_of[6], 71), 0)
    line_table = noise(key_of[5], (L, W), (L * CELLS // RAYS) ** -0.5, 0.0234375, ((1, 8),))
    return {"sources": sources, "density": density, "temp_bins": temp_bins, "ray_index": ray_index, "rate_tables": rate_tables, "line_table": line_table}


def iterate_levels(src_rows, den_rows, table):
    den_col = den_rows[:, None].astype(jnp.float32)
    src_wide = src_rows.astype(jnp.float32)
    first = (den_col * jnp.dot(src_rows, table, preferred_element_type=jnp.float32) + src_wide).astype(jnp.bfloat16)
    second = (den_col * jnp.dot(first, table, preferred_element_type=jnp.float32) + src_wide).astype(jnp.bfloat16)
    return second


def reference(sources, density, temp_bins, ray_index, rate_tables, line_table):
    cell_count = sources.shape[0]
    level_count = sources.shape[1]
    bin_count = rate_tables.shape[0]
    room = N_BIN * N_WAVE * CAP
    bin_of = temp_bins[:, 0].astype(jnp.int32)
    order_cells = jnp.argsort(bin_of, stable=True).astype(jnp.int32)
    sorted_bins = bin_of[order_cells]
    counts = jax.ops.segment_sum(jnp.ones_like(sorted_bins), sorted_bins, num_segments=bin_count)
    starts = (jnp.cumsum(counts) - counts).astype(jnp.int32)
    position = jnp.arange(cell_count, dtype=jnp.int32) - starts[sorted_bins]
    slot_index = (sorted_bins * room + position).astype(jnp.int32)
    src_buffer = jnp.zeros((bin_count * room, level_count), sources.dtype).at[slot_index].set(sources[order_cells])
    den_buffer = jnp.zeros((bin_count * room,), density.dtype).at[slot_index].set(density[order_cells])

    def per_bin(inputs):
        src_rows, den_rows, table = inputs
        return iterate_levels(src_rows, den_rows, table)

    pops_buffer = lax.map(per_bin, (src_buffer.reshape(bin_count, room, level_count), den_buffer.reshape(bin_count, room), rate_tables))
    pops_buffer = pops_buffer.reshape(bin_count * room, level_count)
    populations = jnp.zeros_like(sources).at[order_cells].set(pops_buffer[slot_index])
    ray_sums = jax.ops.segment_sum(populations.astype(jnp.float32), ray_index, num_segments=RAYS)
    return jnp.dot(ray_sums, line_table.astype(jnp.float32), precision=lax.Precision.HIGHEST, preferred_element_type=jnp.float32)
```

```python
import jax
import jax.numpy as jnp
from jax import lax
from jax.experimental import pallas as pl
from jax.experimental.pallas import tpu as pltpu
from jax.sharding import PartitionSpec as P

MESH = pl.DeviceIdType.MESH
F32 = jnp.float32
BF16 = jnp.bfloat16
N_BIN = 64
N_WAVE = 8
SIDE = 8
CAP = 16
CELLS = 512
LEVELS = 256
RAYS = 1024
CHUNKS = 4
PER = N_BIN // CHUNKS
ROWS = PER * CAP


def iota(shape, dim):
    return lax.broadcasted_iota(jnp.int32, shape, dim)


def nt(a, b):
    return lax.dot_general(a, b, (((1,), (1,)), ((), ())), preferred_element_type=F32)


def mm(a, b):
    return jnp.dot(a, b, preferred_element_type=F32)


def as_row(ref):
    v = ref[...]
    return jnp.concatenate([v[i : i + 1, :] for i in range(v.shape[0])], axis=1)


def kernel(
    src_ref, den_ref, bins_ref, ray_ref, tab_ref, out_ref,
    send, esend, recv, erecv, acc, sbuf, crecv, xsend, xrecv, ysend, yrecv, asend, arecv,
    s_sem, e_ssem, r_sem, e_rsem, c_ssem, c_rsem, x_ssem, x_rsem, y_ssem, y_rsem, a_ssem, a_rsem,
):
    me = lax.axis_index("bin")
    wave = lax.axis_index("wave")
    mz, my = me // SIDE, lax.rem(me, SIDE)
    mx, core = wave // 2, lax.rem(wave, 2)

    def peer(i):
        tz = lax.rem(mz + i // SIDE, SIDE)
        ty = lax.rem(my + lax.rem(i, SIDE), SIDE)
        return tz * SIDE + ty

    barrier = pltpu.get_barrier_semaphore()

    @pl.loop(1, N_BIN)
    def _(i):
        pl.semaphore_signal(barrier, inc=1, device_id=(peer(i), wave), device_id_type=MESH)

    @pl.loop(1, N_WAVE)
    def _(i):
        pl.semaphore_signal(
            barrier, inc=1, device_id=(me, lax.rem(wave + i, N_WAVE)), device_id_type=MESH
        )

    bins = as_row(bins_ref)
    den = as_row(den_ref)
    ray = as_row(ray_ref)
    code = ((ray & 15) >> 1) * (2 * N_BIN) + (ray >> 4) * 2 + (ray & 1)
    high = (code >> 5).astype(F32)
    low = (code & 31).astype(F32)
    member = jnp.where(iota((N_BIN, CELLS), 0) == bins, 1.0, 0.0)
    upper = jnp.where(iota((CELLS, CELLS), 0) <= iota((CELLS, CELLS), 1), 1.0, 0.0).astype(BF16)
    rank = mm(member.astype(BF16), upper)
    pos = (jnp.sum(rank * member, axis=0, keepdims=True) - 1.0).astype(jnp.int32)
    slot = bins * CAP + pos
    lane = iota((128, CELLS), 0)
    extras = jnp.zeros((N_BIN, 128), F32)
    for k, value in enumerate((den, high, low)):
        place = jnp.where(lane == pos + k * CAP, 1.0, 0.0).astype(BF16)
        extras = extras + nt((member * value).astype(BF16), place)
    for b in range(N_BIN):
        esend[b] = extras[b : b + 1, :]

    @pl.loop(0, CHUNKS)
    def _(c):
        hot = jnp.where(iota((ROWS, CELLS), 0) + c * ROWS == slot, 1.0, 0.0).astype(BF16)
        packed = mm(hot, src_ref[...]).astype(BF16)
        send[pl.ds(c * PER, PER)] = packed.reshape(PER, CAP, LEVELS)

    acc[...] = jnp.zeros_like(acc)
    pl.semaphore_wait(barrier, N_BIN + N_WAVE - 2)

    @pl.loop(1, N_BIN)
    def _(i):
        to = peer(i)
        pltpu.make_async_remote_copy(
            src_ref=esend.at[to], dst_ref=erecv.at[me], send_sem=e_ssem, recv_sem=e_rsem,
            device_id=(to, wave), device_id_type=MESH,
        ).start()
        pltpu.make_async_remote_copy(
            src_ref=send.at[to], dst_ref=recv.at[me], send_sem=s_sem, recv_sem=r_sem.at[me // PER],
            device_id=(to, wave), device_id_type=MESH,
        ).start()

    pltpu.make_async_copy(esend.at[me], erecv.at[me], e_rsem).start()
    pltpu.make_async_copy(send.at[me], recv.at[me], r_sem.at[me // PER]).start()
    pltpu.make_async_copy(erecv, erecv, e_rsem).wait()

    ones = jnp.ones((128, LEVELS), BF16)
    ones8 = jnp.ones((8, 128), BF16)

    @pl.loop(0, CHUNKS)
    def _(k):
        c = lax.rem(me // PER + k, CHUNKS)
        block = pl.ds(c * PER, PER)
        pltpu.make_async_copy(recv.at[block], recv.at[block], r_sem.at[c]).wait()
        extra = jnp.broadcast_to(erecv[block], (PER, CAP, 128)).reshape(ROWS, 128)
        lanes = iota((ROWS, 128), 1)
        own = iota((ROWS, 128), 0) & (CAP - 1)
        dens = mm(jnp.where(lanes == own, extra, 0.0).astype(BF16), ones)
        coded = jnp.where(
            lanes == own + CAP, extra * 32.0, jnp.where(lanes == own + 2 * CAP, extra, 0.0)
        )
        rays = nt(ones8, coded.astype(BF16))[0:1, :].astype(jnp.int32)
        rows = recv[block].reshape(ROWS, LEVELS)
        wide = rows.astype(F32)
        table = tab_ref[...]
        first = (dens * mm(rows, table) + wide).astype(BF16)
        pops = (dens * mm(first, table) + wide).astype(BF16)
        hot = jnp.where(iota((RAYS, ROWS), 0) == rays, 1.0, 0.0).astype(BF16)
        acc[...] += mm(hot, pops)

    block_rows = RAYS // N_WAVE
    sibling = mx * 2 + 1 - core

    def pair_copy(i):
        tx = lax.rem(mx + i, 4)
        return tx, pltpu.make_async_remote_copy(
            src_ref=sbuf.at[tx], dst_ref=crecv.at[tx], send_sem=c_ssem.at[tx],
            recv_sem=c_rsem.at[tx], device_id=(me, sibling), device_id_type=MESH,
        )

    def x_copy(i):
        tx = lax.rem(mx + i, 4)
        return pltpu.make_async_remote_copy(
            src_ref=xsend.at[tx], dst_ref=xrecv.at[i - 1], send_sem=x_ssem.at[i - 1],
            recv_sem=x_rsem.at[i - 1], device_id=(me, tx * 2 + core), device_id_type=MESH,
        )

    for i in (2, 1, 3, 0):
        tx, copy = pair_copy(i)
        start = pl.multiple_of((tx * 2 + 1 - core) * block_rows, block_rows)
        sbuf[tx] = acc[pl.ds(start, block_rows), :].astype(BF16)
        copy.start()
    total = None
    for i in (2, 1, 3, 0):
        tx, copy = pair_copy(i)
        copy.wait_recv()
        start = pl.multiple_of((tx * 2 + core) * block_rows, block_rows)
        total = acc[pl.ds(start, block_rows), :] + crecv[tx].astype(F32)
        if i != 0:
            xsend[tx] = total.astype(BF16)
            x_copy(i).start()
    for i in (1, 3, 2):
        x_copy(i).wait_recv()
        total = total + xrecv[i - 1].astype(F32)

    for b in range(N_BIN):
        ysend[b] = total[2 * b : 2 * b + 2, :]

    @pl.loop(1, N_BIN)
    def _(i):
        to = peer(i)
        pltpu.make_async_remote_copy(
            src_ref=ysend.at[to], dst_ref=yrecv.at[me], send_sem=y_ssem, recv_sem=y_rsem,
            device_id=(to, wave), device_id_type=MESH,
        ).start()

    pltpu.make_async_copy(ysend.at[me], yrecv.at[me], y_rsem).start()
    pltpu.make_async_copy(yrecv, yrecv, y_rsem).wait()
    asend[...] = jnp.sum(yrecv[...], axis=0)

    @pl.loop(1, N_WAVE)
    def _(i):
        pltpu.make_async_remote_copy(
            src_ref=asend, dst_ref=arecv.at[wave], send_sem=a_ssem, recv_sem=a_rsem,
            device_id=(me, lax.rem(wave + i, N_WAVE)), device_id_type=MESH,
        ).start()

    pltpu.make_async_copy(asend, arecv.at[wave], a_rsem).start()
    pltpu.make_async_copy(arecv, arecv, a_rsem).wait()
    for w in range(N_WAVE):
        out_ref[2 * w : 2 * w + 2, :] = arecv[w]

    rest = pl.ds(0, N_BIN - 1)
    pltpu.make_async_copy(esend.at[rest], esend.at[rest], e_ssem).wait()
    pltpu.make_async_copy(send.at[rest], send.at[rest], s_sem).wait()
    for i in (2, 1, 3, 0):
        pair_copy(i)[1].wait_send()
    for i in (1, 2, 3):
        x_copy(i).wait_send()
    pltpu.make_async_copy(ysend.at[rest], ysend.at[rest], y_ssem).wait()
    others = pl.ds(0, N_WAVE - 1)
    pltpu.make_async_copy(arecv.at[others], arecv.at[others], a_ssem).wait()


def per_device(sources, density, temp_bins, ray_index, rate_tables, line_table):
    vmem = pl.BlockSpec(memory_space=pltpu.VMEM)
    dma = pltpu.SemaphoreType.DMA
    block = RAYS // N_WAVE
    whole_rays = pl.pallas_call(
        kernel,
        out_shape=jax.ShapeDtypeStruct((RAYS // N_BIN, LEVELS), F32),
        in_specs=[vmem] * 5,
        out_specs=vmem,
        scratch_shapes=[
            pltpu.VMEM((N_BIN, CAP, LEVELS), BF16),
            pltpu.VMEM((N_BIN, 1, 128), F32),
            pltpu.VMEM((N_BIN, CAP, LEVELS), BF16),
            pltpu.VMEM((N_BIN, 1, 128), F32),
            pltpu.VMEM((RAYS, LEVELS), F32),
            pltpu.VMEM((4, block, LEVELS), BF16),
            pltpu.VMEM((4, block, LEVELS), BF16),
            pltpu.VMEM((4, block, LEVELS), BF16),
            pltpu.VMEM((3, block, LEVELS), BF16),
            pltpu.VMEM((N_BIN, 2, LEVELS), F32),
            pltpu.VMEM((N_BIN, 2, LEVELS), F32),
            pltpu.VMEM((2, LEVELS), F32),
            pltpu.VMEM((N_WAVE, 2, LEVELS), F32),
            dma, dma, dma((CHUNKS,)), dma, dma((4,)), dma((4,)), dma((3,)), dma((3,)),
            dma, dma, dma, dma,
        ],
        compiler_params=pltpu.CompilerParams(collective_id=0, has_side_effects=True),
        name="populations",
    )(
        sources,
        density.astype(F32).reshape(4, 128),
        temp_bins.reshape(4, 128),
        ray_index.reshape(4, 128),
        rate_tables[0],
    )
    return jnp.dot(
        whole_rays,
        line_table.astype(F32),
        precision=lax.Precision.HIGHEST,
        preferred_element_type=F32,
    )


def solution(mesh):
    in_specs = (
        P(("bin", "wave"), None),
        P(("bin", "wave")),
        P(("bin", "wave"), None),
        P(("bin", "wave")),
        P("bin", None, None),
        P(None, "wave"),
    )
    return jax.shard_map(
        per_device, mesh=mesh, in_specs=in_specs, out_specs=P("bin", "wave"), check_vma=False
    )
```

```python
import jax
import jax.numpy as jnp
from jax import lax
from jax.experimental import pallas as pl
from jax.experimental.pallas import tpu as pltpu
from jax.sharding import PartitionSpec as P

MESH = pl.DeviceIdType.MESH
F32 = jnp.float32
BF16 = jnp.bfloat16
N_BIN = 64
N_WAVE = 8
SIDE = 8
CAP = 16
CELLS = 512
LEVELS = 256
RAYS = 1024
CHUNKS = 4
PER = N_BIN // CHUNKS
ROWS = PER * CAP


def turned(offset):
    return offset[1], (-offset[0]) % SIDE


def reach(offset):
    return sum(min(d, SIDE - d) for d in offset)


def far_first():
    order = []
    offsets = [(dz, dy) for dz in range(SIDE) for dy in range(SIDE)][1:]
    for offset in sorted(offsets, key=lambda o: (-reach(o), o)):
        for _ in range(4):
            if offset not in order:
                order.append(offset)
            offset = turned(offset)
    return order


ORDER = far_first()


def iota(shape, dim):
    return lax.broadcasted_iota(jnp.int32, shape, dim)


def nt(a, b):
    return lax.dot_general(a, b, (((1,), (1,)), ((), ())), preferred_element_type=F32)


def mm(a, b):
    return jnp.dot(a, b, preferred_element_type=F32)


def as_row(ref, dtype=jnp.int32):
    v = ref[...].astype(dtype)
    return jnp.concatenate([v[i : i + 1, :] for i in range(v.shape[0])], axis=1)


def kernel(
    src_hbm, den_ref, bins_ref, ray_ref, tab_hbm, out_ref,
    src_ref, tab_ref, load_sem,
       send, esend, recv, erecv, acc, sbuf, crecv, xsend, xrecv, ysend, yrecv, asend, arecv,
    s_sem, e_ssem, r_sem, e_rsem, c_ssem, c_rsem, x_ssem, x_rsem, y_ssem, y_rsem, a_ssem, a_rsem,
):
    me = lax.axis_index("bin")
    wave = lax.axis_index("wave")
    mz, my = me // SIDE, lax.rem(me, SIDE)
    mx, core = wave // 2, lax.rem(wave, 2)

    def peer(offset):
        return ((mz + offset[0]) & (SIDE - 1)) * SIDE + ((my + offset[1]) & (SIDE - 1))

    barrier = pltpu.get_barrier_semaphore()

    for offset in ORDER:
        pl.semaphore_signal(barrier, inc=1, device_id=(peer(offset), wave), device_id_type=MESH)
    for i in range(1, N_WAVE):
        pl.semaphore_signal(
            barrier, inc=1, device_id=(me, (wave + i) & (N_WAVE - 1)), device_id_type=MESH
        )
    load_src = pltpu.make_async_copy(src_hbm, src_ref, load_sem.at[0])
    load_tab = pltpu.make_async_copy(tab_hbm.at[0], tab_ref, load_sem.at[1])
    load_src.start()
    load_tab.start()

    bins = as_row(bins_ref)
    den = as_row(den_ref, F32)
    ray = as_row(ray_ref)
    code = ((ray & 15) >> 1) * (2 * N_BIN) + (ray >> 4) * 2 + (ray & 1)
    high = (code >> 5).astype(F32)
    low = (code & 31).astype(F32)
    member = jnp.where(iota((N_BIN, CELLS), 0) == bins, 1.0, 0.0)
    upper = jnp.where(iota((CELLS, CELLS), 0) <= iota((CELLS, CELLS), 1), 1.0, 0.0).astype(BF16)
    rank = mm(member.astype(BF16), upper)
    pos = (jnp.sum(rank * member, axis=0, keepdims=True) - 1.0).astype(jnp.int32)
    slot = bins * CAP + pos
    lane = iota((128, CELLS), 0)
    extras = jnp.zeros((N_BIN, 128), F32)
    for k, value in enumerate((den, high, low)):
        place = jnp.where(lane == pos + k * CAP, 1.0, 0.0).astype(BF16)
        extras = extras + nt((member * value).astype(BF16), place)
    for b in range(N_BIN):
        esend[b] = extras[b : b + 1, :]

    load_src.wait()

    @pl.loop(0, CHUNKS)
    def _(c):
        hot = jnp.where(iota((ROWS, CELLS), 0) + c * ROWS == slot, 1.0, 0.0).astype(BF16)
        packed = mm(hot, src_ref[...]).astype(BF16)
        send[pl.ds(c * PER, PER)] = packed.reshape(PER, CAP, LEVELS)

    acc[...] = jnp.zeros_like(acc)
    pl.semaphore_wait(barrier, N_BIN + N_WAVE - 2)

    for offset in ORDER:
        to = peer(offset)
        pltpu.make_async_remote_copy(
            src_ref=esend.at[to], dst_ref=erecv.at[me], send_sem=e_ssem, recv_sem=e_rsem,
            device_id=(to, wave), device_id_type=MESH,
        ).start()
        pltpu.make_async_remote_copy(
            src_ref=send.at[to], dst_ref=recv.at[me], send_sem=s_sem, recv_sem=r_sem.at[me // PER],
            device_id=(to, wave), device_id_type=MESH,
        ).start()

    pltpu.make_async_copy(esend.at[me], erecv.at[me], e_rsem).start()
    pltpu.make_async_copy(send.at[me], recv.at[me], r_sem.at[me // PER]).start()
    load_tab.wait()
    pltpu.make_async_copy(erecv, erecv, e_rsem).wait()

    ones = jnp.ones((128, LEVELS), BF16)
    ones8 = jnp.ones((8, 128), BF16)

    @pl.loop(0, CHUNKS)
    def _(k):
        c = lax.rem(me // PER + k, CHUNKS)
        block = pl.ds(c * PER, PER)
        pltpu.make_async_copy(recv.at[block], recv.at[block], r_sem.at[c]).wait()
        extra = jnp.broadcast_to(erecv[block], (PER, CAP, 128)).reshape(ROWS, 128)
        lanes = iota((ROWS, 128), 1)
        own = iota((ROWS, 128), 0) & (CAP - 1)
        dens = mm(jnp.where(lanes == own, extra, 0.0).astype(BF16), ones)
        coded = jnp.where(
            lanes == own + CAP, extra * 32.0, jnp.where(lanes == own + 2 * CAP, extra, 0.0)
        )
        rays = nt(ones8, coded.astype(BF16))[0:1, :].astype(jnp.int32)
        rows = recv[block].reshape(ROWS, LEVELS)
        wide = rows.astype(F32)
        table = tab_ref[...]
        first = (dens * mm(rows, table) + wide).astype(BF16)
        pops = (dens * mm(first, table) + wide).astype(BF16)
        hot = jnp.where(iota((RAYS, ROWS), 0) == rays, 1.0, 0.0).astype(BF16)
        acc[...] += mm(hot, pops)

    block_rows = RAYS // N_WAVE
    sibling = mx * 2 + 1 - core

    def pair_copy(i):
        tx = lax.rem(mx + i, 4)
        return tx, pltpu.make_async_remote_copy(
            src_ref=sbuf.at[tx], dst_ref=crecv.at[tx], send_sem=c_ssem.at[tx],
            recv_sem=c_rsem.at[tx], device_id=(me, sibling), device_id_type=MESH,
        )

    def x_copy(i):
        tx = lax.rem(mx + i, 4)
        return pltpu.make_async_remote_copy(
            src_ref=xsend.at[tx], dst_ref=xrecv.at[i - 1], send_sem=x_ssem.at[i - 1],
            recv_sem=x_rsem.at[i - 1], device_id=(me, tx * 2 + core), device_id_type=MESH,
        )

    for i in (2, 1, 3, 0):
        tx, copy = pair_copy(i)
        start = pl.multiple_of((tx * 2 + 1 - core) * block_rows, block_rows)
        sbuf[tx] = acc[pl.ds(start, block_rows), :].astype(BF16)
        copy.start()
    total = None
    for i in (2, 1, 3, 0):
        tx, copy = pair_copy(i)
        copy.wait_recv()
        start = pl.multiple_of((tx * 2 + core) * block_rows, block_rows)
        total = acc[pl.ds(start, block_rows), :] + crecv[tx].astype(F32)
        if i != 0:
            xsend[tx] = total.astype(BF16)
            x_copy(i).start()
    for i in (1, 3, 2):
        x_copy(i).wait_recv()
        total = total + xrecv[i - 1].astype(F32)

    total = total.astype(BF16)
    for b in range(N_BIN):
        ysend[b] = total[2 * b : 2 * b + 2, :]

    for offset in ORDER:
        to = peer(offset)
        pltpu.make_async_remote_copy(
            src_ref=ysend.at[to], dst_ref=yrecv.at[me], send_sem=y_ssem, recv_sem=y_rsem,
            device_id=(to, wave), device_id_type=MESH,
        ).start()

    pltpu.make_async_copy(ysend.at[me], yrecv.at[me], y_rsem).start()
    pltpu.make_async_copy(yrecv, yrecv, y_rsem).wait()
    asend[...] = jnp.sum(yrecv[...].astype(F32), axis=0)

    @pl.loop(1, N_WAVE)
    def _(i):
        pltpu.make_async_remote_copy(
            src_ref=asend, dst_ref=arecv.at[wave], send_sem=a_ssem, recv_sem=a_rsem,
            device_id=(me, lax.rem(wave + i, N_WAVE)), device_id_type=MESH,
        ).start()

    pltpu.make_async_copy(asend, arecv.at[wave], a_rsem).start()
    pltpu.make_async_copy(arecv, arecv, a_rsem).wait()
    for w in range(N_WAVE):
        out_ref[2 * w : 2 * w + 2, :] = arecv[w]

    rest = pl.ds(0, N_BIN - 1)
    pltpu.make_async_copy(esend.at[rest], esend.at[rest], e_ssem).wait()
    pltpu.make_async_copy(send.at[rest], send.at[rest], s_sem).wait()
    for i in (2, 1, 3, 0):
        pair_copy(i)[1].wait_send()
    for i in (1, 2, 3):
        x_copy(i).wait_send()
    pltpu.make_async_copy(ysend.at[rest], ysend.at[rest], y_ssem).wait()
    others = pl.ds(0, N_WAVE - 1)
    pltpu.make_async_copy(arecv.at[others], arecv.at[others], a_ssem).wait()


def per_device(sources, density, temp_bins, ray_index, rate_tables, line_table):
    vmem = pl.BlockSpec(memory_space=pltpu.VMEM)
    hbm = pl.BlockSpec(memory_space=pl.ANY)
    dma = pltpu.SemaphoreType.DMA
    block = RAYS // N_WAVE
    whole_rays = pl.pallas_call(
        kernel,
        out_shape=jax.ShapeDtypeStruct((RAYS // N_BIN, LEVELS), F32),
        in_specs=[hbm, vmem, vmem, vmem, hbm],
        out_specs=vmem,
        scratch_shapes=[
            pltpu.VMEM((CELLS, LEVELS), BF16),
            pltpu.VMEM((LEVELS, LEVELS), BF16),
            dma((2,)),
            pltpu.VMEM((N_BIN, CAP, LEVELS), BF16),
            pltpu.VMEM((N_BIN, 1, 128), F32),
            pltpu.VMEM((N_BIN, CAP, LEVELS), BF16),
            pltpu.VMEM((N_BIN, 1, 128), F32),
            pltpu.VMEM((RAYS, LEVELS), F32),
            pltpu.VMEM((4, block, LEVELS), BF16),
            pltpu.VMEM((4, block, LEVELS), BF16),
            pltpu.VMEM((4, block, LEVELS), BF16),
            pltpu.VMEM((3, block, LEVELS), BF16),
            pltpu.VMEM((N_BIN, 2, LEVELS), BF16),
            pltpu.VMEM((N_BIN, 2, LEVELS), BF16),
            pltpu.VMEM((2, LEVELS), F32),
            pltpu.VMEM((N_WAVE, 2, LEVELS), F32),
            dma, dma, dma((CHUNKS,)), dma, dma((4,)), dma((4,)), dma((3,)), dma((3,)),
            dma, dma, dma, dma,
        ],
        compiler_params=pltpu.CompilerParams(collective_id=0, has_side_effects=True),
        name="populations",
    )(
        sources,
        density.reshape(4, 128),
        temp_bins.reshape(4, 128),
        ray_index.reshape(4, 128),
        rate_tables,
    )
    return jnp.dot(
        whole_rays,
        line_table.astype(F32),
        precision=lax.Precision.HIGHEST,
        preferred_element_type=F32,
    )


def solution(mesh):
    in_specs = (
        P(("bin", "wave"), None),
        P(("bin", "wave")),
        P(("bin", "wave"), None),
        P(("bin", "wave")),
        P("bin", None, None),
        P(None, "wave"),
    )
    return jax.shard_map(
        per_device, mesh=mesh, in_specs=in_specs, out_specs=P("bin", "wave"), check_vma=False
    )
```

```python
import jax
import jax.numpy as jnp
from jax import lax
from jax.experimental import pallas as pl
from jax.experimental.pallas import tpu as pltpu
from jax.sharding import PartitionSpec as P

MESH = pl.DeviceIdType.MESH
F32 = jnp.float32
BF16 = jnp.bfloat16
N_BIN = 64
N_WAVE = 8
N_X = 4
SIDE = 8
CAP = 16
CELLS = 512
LEVELS = 256
RAYS = 1024
CHUNKS = 4
PER = N_BIN // CHUNKS
ROWS = PER * CAP
PIECES = 4
PIECE_BINS = N_BIN // PIECES
PIECE = RAYS // PIECES
SHARE = PIECE // N_WAVE


def turned(offset):
    return offset[1], (-offset[0]) % SIDE


def reach(offset):
    return sum(min(d, SIDE - d) for d in offset)


def far_first():
    order = []
    offsets = [(dz, dy) for dz in range(SIDE) for dy in range(SIDE)]
    for offset in sorted(offsets, key=lambda o: (-reach(o), o)):
        for _ in range(4):
            if offset not in order:
                order.append(offset)
            offset = turned(offset)
    return order


ORDER = far_first()


def iota(shape, dim):
    return lax.broadcasted_iota(jnp.int32, shape, dim)


def nt(a, b):
    return lax.dot_general(a, b, (((1,), (1,)), ((), ())), preferred_element_type=F32)


def mm(a, b):
    return jnp.dot(a, b, preferred_element_type=F32)


def as_row(ref, dtype=jnp.int32):
    v = ref[...].astype(dtype)
    return jnp.concatenate([v[i : i + 1, :] for i in range(v.shape[0])], axis=1)


def kernel(
    src_hbm, den_hbm, bins_hbm, ray_hbm, tab_hbm, out_any,
    src_ref, den_ref, bins_ref, ray_ref, tab_ref, out_ref, load_sem,
    send, esend, recv, erecv, acc, sbuf, crecv, xsend, xrecv, ysend, yrecv, asend, arecv,
    s_sem, e_ssem, r_sem, e_rsem, c_ssem, c_rsem, x_ssem, x_rsem, y_ssem, y_rsem, a_ssem, a_rsem,
):
    me = lax.axis_index("bin")
    wave = lax.axis_index("wave")
    mz, my = me // SIDE, me & (SIDE - 1)
    mx, core = wave // 2, wave & 1

    def peer(offset):
        return ((mz + offset[0]) & (SIDE - 1)) * SIDE + ((my + offset[1]) & (SIDE - 1))

    loads = [
        pltpu.make_async_copy(given, held, load_sem.at[n])
        for n, (given, held) in enumerate((
            (bins_hbm, bins_ref), (den_hbm, den_ref), (ray_hbm, ray_ref), (src_hbm, src_ref),
            (tab_hbm.at[0], tab_ref),
        ))
    ]
    for load in loads:
        load.start()
    barrier = pltpu.get_barrier_semaphore()
    for offset in ORDER[:-1]:
        pl.semaphore_signal(barrier, inc=1, device_id=(peer(offset), wave), device_id_type=MESH)
    for i in range(1, N_WAVE):
        pl.semaphore_signal(
            barrier, inc=1, device_id=(me, (wave + i) & (N_WAVE - 1)), device_id_type=MESH
        )

    for load in loads[:3]:
        load.wait()
    bins = as_row(bins_ref)
    den = as_row(den_ref, F32)
    ray = as_row(ray_ref)
    code = (ray >> 8) * PIECE + ((ray & 15) >> 1) * SHARE + ((ray >> 4) & 15) * 2 + (ray & 1)
    high = (code >> 5).astype(F32)
    low = (code & 31).astype(F32)
    member = jnp.where(iota((N_BIN, CELLS), 0) == bins, 1.0, 0.0)
    upper = jnp.where(iota((CELLS, CELLS), 0) <= iota((CELLS, CELLS), 1), 1.0, 0.0).astype(BF16)
    rank = mm(member.astype(BF16), upper)
    pos = (jnp.sum(rank * member, axis=0, keepdims=True) - 1.0).astype(jnp.int32)
    slot = bins * CAP + pos
    lane = iota((128, CELLS), 0)
    extras = jnp.zeros((N_BIN, 128), F32)
    for k, value in enumerate((den, high, low)):
        place = jnp.where(lane == pos + k * CAP, 1.0, 0.0).astype(BF16)
        extras = extras + nt((member * value).astype(BF16), place)
    for b in range(N_BIN):
        esend[b] = extras[b : b + 1, :]
    loads[3].wait()

    @pl.loop(0, CHUNKS)
    def _(c):
        hot = jnp.where(iota((ROWS, CELLS), 0) + c * ROWS == slot, 1.0, 0.0).astype(BF16)
        packed = mm(hot, src_ref[...]).astype(BF16)
        send[pl.ds(c * PER, PER)] = packed.reshape(PER, CAP, LEVELS)

    pl.semaphore_wait(barrier, N_BIN + N_WAVE - 2)

    for k, offset in enumerate(ORDER[:-1]):
        to = peer(offset)
        for out, into, s, r in ((esend, erecv, e_ssem, e_rsem), (send, recv, s_sem, r_sem)):
            pltpu.make_async_remote_copy(
                src_ref=out.at[to], dst_ref=into.at[k], send_sem=s, recv_sem=r.at[k // PER],
                device_id=(to, wave), device_id_type=MESH,
            ).start()
    pltpu.make_async_copy(esend.at[me], erecv.at[N_BIN - 1], e_rsem.at[CHUNKS - 1]).start()
    pltpu.make_async_copy(send.at[me], recv.at[N_BIN - 1], r_sem.at[CHUNKS - 1]).start()

    acc[...] = jnp.zeros_like(acc)
    loads[4].wait()
    ones = jnp.ones((128, LEVELS), BF16)
    ones8 = jnp.ones((8, 128), BF16)

    def chunk(c):
        block = pl.ds(c * PER, PER)
        pltpu.make_async_copy(erecv.at[block], erecv.at[block], e_rsem.at[c]).wait()
        pltpu.make_async_copy(recv.at[block], recv.at[block], r_sem.at[c]).wait()
        extra = jnp.broadcast_to(erecv[block], (PER, CAP, 128)).reshape(ROWS, 128)
        lanes = iota((ROWS, 128), 1)
        own = iota((ROWS, 128), 0) & (CAP - 1)
        dens = mm(jnp.where(lanes == own, extra, 0.0).astype(BF16), ones)
        coded = jnp.where(
            lanes == own + CAP, extra * 32.0, jnp.where(lanes == own + 2 * CAP, extra, 0.0)
        )
        rays = nt(ones8, coded.astype(BF16))[0:1, :].astype(jnp.int32)
        rows = recv[block].reshape(ROWS, LEVELS)
        wide = rows.astype(F32)
        table = tab_ref[...]
        first = (dens * mm(rows, table) + wide).astype(BF16)
        pops = (dens * mm(first, table) + wide).astype(BF16)
        return rays, pops

    @pl.loop(0, CHUNKS - 1)
    def _(c):
        rays, pops = chunk(c)
        hot = jnp.where(iota((RAYS, ROWS), 0) == rays, 1.0, 0.0).astype(BF16)
        acc[...] += mm(hot, pops)

    rays, pops = chunk(CHUNKS - 1)

    pieces = [((mz >> 1) + k) & (PIECES - 1) for k in (2, 1, 3, 0)]

    def pair_copy(n):
        return pltpu.make_async_remote_copy(
            src_ref=sbuf.at[n], dst_ref=crecv.at[n], send_sem=c_ssem.at[n], recv_sem=c_rsem.at[n],
            device_id=(me, mx * 2 + 1 - core), device_id_type=MESH,
        )

    def x_copy(n, i):
        return pltpu.make_async_remote_copy(
            src_ref=xsend.at[n, i - 1], dst_ref=xrecv.at[n, i - 1], send_sem=x_ssem.at[n, i - 1],
            recv_sem=x_rsem.at[n, i - 1],
            device_id=(me, ((mx + i) & (N_X - 1)) * 2 + core), device_id_type=MESH,
        )

    def share(piece, member_x, member_core):
        at = piece * PIECE + (member_x * 2 + member_core) * SHARE
        return pl.ds(pl.multiple_of(at, SHARE), SHARE)

    def sum_cells(n):
        piece = pieces[n]
        here = pl.ds(pl.multiple_of(piece * PIECE, PIECE), PIECE)
        hot = jnp.where(iota((PIECE, ROWS), 0) + piece * PIECE == rays, 1.0, 0.0).astype(BF16)
        acc[here, :] += mm(hot, pops)
        for x in range(N_X):
            sbuf[n, x] = acc[share(piece, x, 1 - core), :].astype(BF16)
        pair_copy(n).start()

    def sum_pair(n):
        pair_copy(n).wait_recv()
        for i in (2, 1, 3):
            x = (mx + i) & (N_X - 1)
            both = acc[share(pieces[n], x, core), :] + crecv[n, x].astype(F32)
            xsend[n, i - 1] = both.astype(BF16)
            x_copy(n, i).start()

    def sum_x(n):
        piece = pieces[n]
        total = acc[share(piece, mx, core), :] + crecv[n, mx].astype(F32)
        for i in (1, 3, 2):
            x_copy(n, i).wait_recv()
            total = total + xrecv[n, i - 1].astype(F32)
        total = total.astype(BF16)
        for j in range(PIECE_BINS):
            ysend[piece * PIECE_BINS + j] = total[2 * j : 2 * j + 2, :]

        @pl.loop(0, PIECE_BINS)
        def _(j):
            to = piece * PIECE_BINS + ((me + j) & (PIECE_BINS - 1))

            @pl.when(to != me)
            def _():
                pltpu.make_async_remote_copy(
                    src_ref=ysend.at[to], dst_ref=yrecv.at[me], send_sem=y_ssem, recv_sem=y_rsem,
                    device_id=(to, wave), device_id_type=MESH,
                ).start()

    sum_cells(0)
    sum_cells(1)
    sum_pair(0)
    sum_cells(2)
    sum_pair(1)
    sum_cells(3)
    sum_pair(2)
    sum_pair(3)
    for n in range(PIECES):
        sum_x(n)

    pltpu.make_async_copy(ysend.at[me], yrecv.at[me], y_rsem).start()
    pltpu.make_async_copy(yrecv, yrecv, y_rsem).wait()
    asend[...] = jnp.sum(yrecv[...].astype(F32), axis=0)
    for i in range(1, N_WAVE):
        pltpu.make_async_remote_copy(
            src_ref=asend, dst_ref=arecv.at[wave], send_sem=a_ssem, recv_sem=a_rsem,
            device_id=(me, (wave + i) & (N_WAVE - 1)), device_id_type=MESH,
        ).start()
    pltpu.make_async_copy(asend, arecv.at[wave], a_rsem).start()

    rest = pl.ds(0, N_BIN - 1)
    pltpu.make_async_copy(esend.at[rest], esend.at[rest], e_ssem).wait()
    pltpu.make_async_copy(send.at[rest], send.at[rest], s_sem).wait()
    for n in range(PIECES):
        pair_copy(n).wait_send()
        for i in (1, 2, 3):
            x_copy(n, i).wait_send()
    pltpu.make_async_copy(ysend.at[rest], ysend.at[rest], y_ssem).wait()

    pltpu.make_async_copy(arecv, arecv, a_rsem).wait()
    for w in range(N_WAVE):
        out_ref[2 * w : 2 * w + 2, :] = arecv[w]
    store = pltpu.make_async_copy(out_ref, out_any, load_sem.at[0])
    store.start()
    others = pl.ds(0, N_WAVE - 1)
    pltpu.make_async_copy(arecv.at[others], arecv.at[others], a_ssem).wait()
    store.wait()


def per_device(sources, density, temp_bins, ray_index, rate_tables, line_table):
    hbm = pl.BlockSpec(memory_space=pltpu.HBM)
    dma = pltpu.SemaphoreType.DMA
    whole_rays = pl.pallas_call(
        kernel,
        out_shape=jax.ShapeDtypeStruct((RAYS // N_BIN, LEVELS), F32),
        in_specs=[hbm] * 5,
        out_specs=pl.BlockSpec(memory_space=pl.ANY),
        scratch_shapes=[
            pltpu.VMEM((CELLS, LEVELS), BF16),
            pltpu.VMEM((CELLS // 128, 128), BF16),
            pltpu.VMEM((CELLS // 128, 128), jnp.int32),
            pltpu.VMEM((CELLS // 128, 128), jnp.int32),
            pltpu.VMEM((LEVELS, LEVELS), BF16),
            pltpu.VMEM((RAYS // N_BIN, LEVELS), F32),
            dma((5,)),
            pltpu.VMEM((N_BIN, CAP, LEVELS), BF16),
            pltpu.VMEM((N_BIN, 1, 128), F32),
            pltpu.VMEM((N_BIN, CAP, LEVELS), BF16),
            pltpu.VMEM((N_BIN, 1, 128), F32),
            pltpu.VMEM((RAYS, LEVELS), F32),
            pltpu.VMEM((PIECES, N_X, SHARE, LEVELS), BF16),
            pltpu.VMEM((PIECES, N_X, SHARE, LEVELS), BF16),
            pltpu.VMEM((PIECES, N_X - 1, SHARE, LEVELS), BF16),
            pltpu.VMEM((PIECES, N_X - 1, SHARE, LEVELS), BF16),
            pltpu.VMEM((N_BIN, 2, LEVELS), BF16),
            pltpu.VMEM((N_BIN, 2, LEVELS), BF16),
            pltpu.VMEM((2, LEVELS), F32),
            pltpu.VMEM((N_WAVE, 2, LEVELS), F32),
            dma, dma, dma((CHUNKS,)), dma((CHUNKS,)), dma((PIECES,)), dma((PIECES,)),
            dma((PIECES, N_X - 1)), dma((PIECES, N_X - 1)),
            dma, dma, dma, dma,
        ],
        compiler_params=pltpu.CompilerParams(
            collective_id=0, has_side_effects=True, vmem_limit_bytes=24 * 1024 * 1024
        ),
        name="populations",
    )(*(pltpu.with_memory_space_constraint(a, pltpu.HBM) for a in (
        sources,
        density.reshape(4, 128),
        temp_bins.reshape(4, 128),
        ray_index.reshape(4, 128),
        rate_tables,
    )))
    return jnp.dot(
        whole_rays,
        line_table.astype(F32),
        precision=lax.Precision.HIGHEST,
        preferred_element_type=F32,
    )


def solution(mesh):
    in_specs = (
        P(("bin", "wave"), None),
        P(("bin", "wave")),
        P(("bin", "wave"), None),
        P(("bin", "wave")),
        P("bin", None, None),
        P(None, "wave"),
    )
    return jax.shard_map(
        per_device, mesh=mesh, in_specs=in_specs, out_specs=P("bin", "wave"), check_vma=False
    )
```

```python
import jax
import jax.numpy as jnp
from jax import lax
from jax.experimental import pallas as pl
from jax.experimental.pallas import tpu as pltpu
from jax.sharding import PartitionSpec as P

MESH = pl.DeviceIdType.MESH
F32 = jnp.float32
BF16 = jnp.bfloat16
N_BIN = 64
N_WAVE = 8
N_X = 4
SIDE = 8
CAP = 16
CELLS = 512
LEVELS = 256
RAYS = 1024
CHUNKS = 4
PER = N_BIN // CHUNKS
ROWS = PER * CAP
PIECES = 4
PIECE_BINS = N_BIN // PIECES
PIECE = RAYS // PIECES
SHARE = PIECE // N_WAVE


STEPS = ((1, 0), (0, -1), (-1, 0), (0, 1))


def signed(d):
    return (d + SIDE // 2 - 1) % SIDE - SIDE // 2 + 1


def reach(offset):
    return sum(abs(signed(d)) for d in offset)


def turned(offset):
    return offset[1], (-offset[0]) % SIDE


def before(offset, step):
    return (offset[0] - step[0]) % SIDE, (offset[1] - step[1]) % SIDE


def plan():
    half = SIDE // 2
    last = [(half, half), (0, half), (half, 0), (0, 0)]
    groups, seen = [], set(last)
    offsets = [(dz, dy) for dz in range(SIDE) for dy in range(SIDE)]
    for offset in sorted(offsets, key=lambda o: (-reach(o), o)):
        if offset in seen:
            continue
        dz, dy = signed(offset[0]), signed(offset[1])
        along = (1 if dz > 0 else -1, 0) if abs(dz) >= abs(dy) else (0, 1 if dy > 0 else -1)
        group = [None] * 4
        for n in range(4):
            group[(STEPS.index(along) + n) % 4] = offset
            seen.add(offset)
            offset = turned(offset)
        groups.append(group)
    return groups + [last]


GROUPS = plan()
PER_CHUNK = len(GROUPS) // CHUNKS
SLOTS = []
for c in range(CHUNKS):
    for d, step in enumerate(STEPS):
        for group in GROUPS[c * PER_CHUNK : (c + 1) * PER_CHUNK]:
            owner = group[d]
            SLOTS.append((owner, before(owner, step) if owner != (0, 0) else owner))


SEND = sorted(
    range(N_BIN), key=lambda k: (-reach(SLOTS[k][1]), k // PER, k % PER_CHUNK, k % PER // PER_CHUNK)
)
PLANE = [owner for owner, _ in SLOTS if owner != (0, 0)]


def iota(shape, dim):
    return lax.broadcasted_iota(jnp.int32, shape, dim)


def nt(a, b):
    return lax.dot_general(a, b, (((1,), (1,)), ((), ())), preferred_element_type=F32)


def mm(a, b):
    return jnp.dot(a, b, preferred_element_type=F32)


def as_row(ref, dtype=jnp.int32):
    v = ref[...].astype(dtype)
    return jnp.concatenate([v[i : i + 1, :] for i in range(v.shape[0])], axis=1)


def kernel(
    src_hbm, den_hbm, bins_hbm, ray_hbm, tab_hbm, out_any,
    src_ref, den_ref, bins_ref, ray_ref, tab_ref, out_ref, load_sem,
    send, esend, recv, erecv, acc, sbuf, crecv, xsend, xrecv, ysend, yrecv, asend, arecv,
    near, t_ssem, t_rsem, met, s_sem, e_ssem, r_sem, e_rsem, c_ssem, c_rsem, x_ssem, x_rsem, y_ssem, y_rsem, a_ssem, a_rsem,
):
    me = lax.axis_index("bin")
    wave = lax.axis_index("wave")
    mz, my = me // SIDE, me & (SIDE - 1)
    mx, core = wave // 2, wave & 1

    def peer(offset):
        return ((mz + offset[0]) & (SIDE - 1)) * SIDE + ((my + offset[1]) & (SIDE - 1))

    loads = [
        pltpu.make_async_copy(given, held, load_sem.at[n])
        for n, (given, held) in enumerate((
            (bins_hbm, bins_ref), (den_hbm, den_ref), (ray_hbm, ray_ref), (src_hbm, src_ref),
            (tab_hbm.at[0], tab_ref),
        ))
    ]
    for load in loads:
        load.start()
    barrier = pltpu.get_barrier_semaphore()

    def greet(bin_at, wave_at):
        pl.semaphore_signal(barrier, inc=1, device_id=(bin_at, wave_at), device_id_type=MESH)

    first_core = mx * 2
    for offset in sorted(PLANE, key=lambda o: -reach(o)):
        greet(peer(offset), first_core)
    for i in range(1, N_X):
        greet(me, ((mx + i) & (N_X - 1)) * 2)
    for step in STEPS:
        greet(peer(step), first_core + 1)
    greet(me, first_core + 1 - core)

    def table_copy(d):
        back = (-STEPS[d][0], -STEPS[d][1])
        return pltpu.make_async_remote_copy(
            src_ref=tab_ref, dst_ref=near.at[d], send_sem=t_ssem.at[d], recv_sem=t_rsem.at[d],
            device_id=(peer(back), wave), device_id_type=MESH,
        )

    def ship():
        for k in SEND:
            owner, host = SLOTS[k]
            own, to = peer(owner), peer(host)
            for out, into, s, r in ((esend, erecv, e_ssem, e_rsem), (send, recv, s_sem, r_sem)):
                if host == (0, 0):
                    pltpu.make_async_copy(out.at[own], into.at[k], r.at[k // PER]).start()
                else:
                    pltpu.make_async_remote_copy(
                        src_ref=out.at[own], dst_ref=into.at[k], send_sem=s,
                        recv_sem=r.at[k // PER], device_id=(to, wave), device_id_type=MESH,
                    ).start()

    @pl.when(core == 1)
    def _():
        pl.semaphore_wait(barrier, 2 * len(STEPS) + 1)
        pl.semaphore_signal(met.at[0], inc=1, device_id=(me, first_core), device_id_type=MESH)

    @pl.when(core == 0)
    def _():
        pl.semaphore_wait(met.at[0], 1)

    loads[4].wait()
    for d in range(4):
        table_copy(d).start()

    for load in loads[:3]:
        load.wait()
    bins = as_row(bins_ref)
    den = as_row(den_ref, F32)
    ray = as_row(ray_ref)
    code = (ray >> 8) * PIECE + ((ray & 15) >> 1) * SHARE + ((ray >> 4) & 15) * 2 + (ray & 1)
    high = (code >> 5).astype(F32)
    low = (code & 31).astype(F32)
    member = jnp.where(iota((N_BIN, CELLS), 0) == bins, 1.0, 0.0)
    upper = jnp.where(iota((CELLS, CELLS), 0) <= iota((CELLS, CELLS), 1), 1.0, 0.0).astype(BF16)
    rank = mm(member.astype(BF16), upper)
    pos = (jnp.sum(rank * member, axis=0, keepdims=True) - 1.0).astype(jnp.int32)
    slot = bins * CAP + pos
    lane = iota((128, CELLS), 0)
    extras = jnp.zeros((N_BIN, 128), F32)
    for k, value in enumerate((den, high, low)):
        place = jnp.where(lane == pos + k * CAP, 1.0, 0.0).astype(BF16)
        extras = extras + nt((member * value).astype(BF16), place)
    for b in range(N_BIN):
        esend[b] = extras[b : b + 1, :]
    loads[3].wait()

    def pack(c):
        hot = jnp.where(iota((ROWS, CELLS), 0) + c * ROWS == slot, 1.0, 0.0).astype(BF16)
        packed = mm(hot, src_ref[...]).astype(BF16)
        send[pl.ds(c * PER, PER)] = packed.reshape(PER, CAP, LEVELS)

    @pl.loop(0, CHUNKS)
    def _(c):
        pack(c)

    @pl.when(core == 0)
    def _():
        pl.semaphore_wait(barrier, 2 * (N_BIN - 1) + 2 * (N_X - 1) + 1)
        pl.semaphore_signal(met.at[1], inc=1, device_id=(me, first_core + 1), device_id_type=MESH)

    @pl.when(core == 1)
    def _():
        pl.semaphore_wait(met.at[1], 1)

    ship()
    acc[...] = jnp.zeros_like(acc)
    for d in range(4):
        table_copy(d).wait_recv()
    ones = jnp.ones((128, LEVELS), BF16)
    ones8 = jnp.ones((8, 128), BF16)

    quarter = ROWS // 4

    def by_table(rows, last):
        parts = [mm(rows[d * quarter : (d + 1) * quarter], near[d]) for d in range(3)]
        if last:
            parts.append(mm(rows[3 * quarter : ROWS - CAP], near[3]))
            parts.append(mm(rows[ROWS - CAP :], tab_ref[...]))
        else:
            parts.append(mm(rows[3 * quarter :], near[3]))
        return jnp.concatenate(parts, axis=0)

    def chunk(c, last=False):
        block = pl.ds(c * PER, PER)
        pltpu.make_async_copy(erecv.at[block], erecv.at[block], e_rsem.at[c]).wait()
        pltpu.make_async_copy(recv.at[block], recv.at[block], r_sem.at[c]).wait()
        extra = jnp.broadcast_to(erecv[block], (PER, CAP, 128)).reshape(ROWS, 128)
        lanes = iota((ROWS, 128), 1)
        own = iota((ROWS, 128), 0) & (CAP - 1)
        dens = mm(jnp.where(lanes == own, extra, 0.0).astype(BF16), ones)
        coded = jnp.where(
            lanes == own + CAP, extra * 32.0, jnp.where(lanes == own + 2 * CAP, extra, 0.0)
        )
        rays = nt(ones8, coded.astype(BF16))[0:1, :].astype(jnp.int32)
        rows = recv[block].reshape(ROWS, LEVELS)
        wide = rows.astype(F32)
        first = (dens * by_table(rows, last) + wide).astype(BF16)
        pops = (dens * by_table(first, last) + wide).astype(BF16)
        return rays, pops

    @pl.loop(0, CHUNKS - 1)
    def _(c):
        rays, pops = chunk(c)
        hot = jnp.where(iota((RAYS, ROWS), 0) == rays, 1.0, 0.0).astype(BF16)
        acc[...] += mm(hot, pops)

    rays, pops = chunk(CHUNKS - 1, last=True)

    pieces = [((mz >> 1) + k) & (PIECES - 1) for k in (2, 1, 3, 0)]

    def pair_copy(n):
        return pltpu.make_async_remote_copy(
            src_ref=sbuf.at[n], dst_ref=crecv.at[n], send_sem=c_ssem.at[n], recv_sem=c_rsem.at[n],
            device_id=(me, mx * 2 + 1 - core), device_id_type=MESH,
        )

    def x_copy(n, i):
        return pltpu.make_async_remote_copy(
            src_ref=xsend.at[n, i - 1], dst_ref=xrecv.at[n, i - 1], send_sem=x_ssem.at[n, i - 1],
            recv_sem=x_rsem.at[n, i - 1],
            device_id=(me, ((mx + i) & (N_X - 1)) * 2 + core), device_id_type=MESH,
        )

    def share(piece, member_x, member_core):
        at = piece * PIECE + (member_x * 2 + member_core) * SHARE
        return pl.ds(pl.multiple_of(at, SHARE), SHARE)

    def sum_cells(n):
        piece = pieces[n]
        here = pl.ds(pl.multiple_of(piece * PIECE, PIECE), PIECE)
        hot = jnp.where(iota((PIECE, ROWS), 0) + piece * PIECE == rays, 1.0, 0.0).astype(BF16)
        acc[here, :] += mm(hot, pops)
        for x in range(N_X):
            sbuf[n, x] = acc[share(piece, x, 1 - core), :].astype(BF16)
        pair_copy(n).start()

    def sum_pair(n):
        pair_copy(n).wait_recv()
        for i in (2, 1, 3):
            x = (mx + i) & (N_X - 1)
            both = acc[share(pieces[n], x, core), :] + crecv[n, x].astype(F32)
            xsend[n, i - 1] = both.astype(BF16)
            x_copy(n, i).start()

    def sum_x(n):
        piece = pieces[n]
        total = acc[share(piece, mx, core), :] + crecv[n, mx].astype(F32)
        for i in (1, 3, 2):
            x_copy(n, i).wait_recv()
            total = total + xrecv[n, i - 1].astype(F32)
        total = total.astype(BF16)
        for j in range(PIECE_BINS):
            ysend[piece * PIECE_BINS + j] = total[2 * j : 2 * j + 2, :]

        @pl.loop(0, PIECE_BINS)
        def _(j):
            to = piece * PIECE_BINS + ((me + j) & (PIECE_BINS - 1))

            @pl.when(to != me)
            def _():
                pltpu.make_async_remote_copy(
                    src_ref=ysend.at[to], dst_ref=yrecv.at[me], send_sem=y_ssem, recv_sem=y_rsem,
                    device_id=(to, wave), device_id_type=MESH,
                ).start()

    sum_cells(0)
    sum_cells(1)
    sum_pair(0)
    sum_cells(2)
    sum_pair(1)
    sum_cells(3)
    sum_pair(2)
    sum_pair(3)
    for n in range(PIECES):
        sum_x(n)

    pltpu.make_async_copy(ysend.at[me], yrecv.at[me], y_rsem).start()
    pltpu.make_async_copy(yrecv, yrecv, y_rsem).wait()
    asend[...] = jnp.sum(yrecv[...].astype(F32), axis=0)
    for i in range(1, N_WAVE):
        pltpu.make_async_remote_copy(
            src_ref=asend, dst_ref=arecv.at[wave], send_sem=a_ssem, recv_sem=a_rsem,
            device_id=(me, (wave + i) & (N_WAVE - 1)), device_id_type=MESH,
        ).start()
    pltpu.make_async_copy(asend, arecv.at[wave], a_rsem).start()

    for d in range(4):
        table_copy(d).wait_send()
    away = pl.ds(0, sum(host != (0, 0) for _, host in SLOTS))
    pltpu.make_async_copy(esend.at[away], esend.at[away], e_ssem).wait()
    pltpu.make_async_copy(send.at[away], send.at[away], s_sem).wait()
    rest = pl.ds(0, N_BIN - 1)
    for n in range(PIECES):
        pair_copy(n).wait_send()
        for i in (1, 2, 3):
            x_copy(n, i).wait_send()
    pltpu.make_async_copy(ysend.at[rest], ysend.at[rest], y_ssem).wait()

    pltpu.make_async_copy(arecv, arecv, a_rsem).wait()
    for w in range(N_WAVE):
        out_any[2 * w : 2 * w + 2, :] = arecv[w]
    others = pl.ds(0, N_WAVE - 1)
    pltpu.make_async_copy(arecv.at[others], arecv.at[others], a_ssem).wait()


def per_device(sources, density, temp_bins, ray_index, rate_tables, line_table):
    hbm = pl.BlockSpec(memory_space=pltpu.HBM)
    dma = pltpu.SemaphoreType.DMA
    whole_rays = pl.pallas_call(
        kernel,
        out_shape=jax.ShapeDtypeStruct((RAYS // N_BIN, LEVELS), F32),
        in_specs=[hbm] * 5,
        out_specs=pl.BlockSpec(memory_space=pltpu.VMEM),
        scratch_shapes=[
            pltpu.VMEM((CELLS, LEVELS), BF16),
            pltpu.VMEM((CELLS // 128, 128), BF16),
            pltpu.VMEM((CELLS // 128, 128), jnp.int32),
            pltpu.VMEM((CELLS // 128, 128), jnp.int32),
            pltpu.VMEM((LEVELS, LEVELS), BF16),
            pltpu.VMEM((RAYS // N_BIN, LEVELS), F32),
            dma((5,)),
            pltpu.VMEM((N_BIN, CAP, LEVELS), BF16),
            pltpu.VMEM((N_BIN, 1, 128), F32),
            pltpu.VMEM((N_BIN, CAP, LEVELS), BF16),
            pltpu.VMEM((N_BIN, 1, 128), F32),
            pltpu.VMEM((RAYS, LEVELS), F32),
            pltpu.VMEM((PIECES, N_X, SHARE, LEVELS), BF16),
            pltpu.VMEM((PIECES, N_X, SHARE, LEVELS), BF16),
            pltpu.VMEM((PIECES, N_X - 1, SHARE, LEVELS), BF16),
            pltpu.VMEM((PIECES, N_X - 1, SHARE, LEVELS), BF16),
            pltpu.VMEM((N_BIN, 2, LEVELS), BF16),
            pltpu.VMEM((N_BIN, 2, LEVELS), BF16),
            pltpu.VMEM((2, LEVELS), F32),
            pltpu.VMEM((N_WAVE, 2, LEVELS), F32),
            pltpu.VMEM((4, LEVELS, LEVELS), BF16),
            dma((4,)), dma((4,)), pltpu.SemaphoreType.REGULAR((2,)),
            dma, dma, dma((CHUNKS,)), dma((CHUNKS,)), dma((PIECES,)), dma((PIECES,)),
            dma((PIECES, N_X - 1)), dma((PIECES, N_X - 1)),
            dma, dma, dma, dma,
        ],
        compiler_params=pltpu.CompilerParams(
            collective_id=0, has_side_effects=True, vmem_limit_bytes=24 * 1024 * 1024
        ),
        name="populations",
    )(*(pltpu.with_memory_space_constraint(a, pltpu.HBM) for a in (
        sources,
        density.reshape(4, 128),
        temp_bins.reshape(4, 128),
        ray_index.reshape(4, 128),
        rate_tables,
    )))
    return jnp.dot(
        whole_rays,
        line_table.astype(F32),
        precision=lax.Precision.HIGHEST,
        preferred_element_type=F32,
    )


def solution(mesh):
    in_specs = (
        P(("bin", "wave"), None),
        P(("bin", "wave")),
        P(("bin", "wave"), None),
        P(("bin", "wave")),
        P("bin", None, None),
        P(None, "wave"),
    )
    return jax.shard_map(
        per_device, mesh=mesh, in_specs=in_specs, out_specs=P("bin", "wave"), check_vma=False
    )
```

```python
import jax
import jax.numpy as jnp
from jax import lax
from jax.experimental import pallas as pl
from jax.experimental.pallas import tpu as pltpu
from jax.sharding import PartitionSpec as P

MESH = pl.DeviceIdType.MESH
F32 = jnp.float32
BF16 = jnp.bfloat16
N_BIN = 64
N_WAVE = 8
N_X = 4
SIDE = 8
CAP = 16
CELLS = 512
LEVELS = 256
RAYS = 1024
CHUNKS = 4
PER = N_BIN // CHUNKS
ROWS = PER * CAP
PIECES = 4
PIECE_BINS = N_BIN // PIECES
PIECE = RAYS // PIECES
SHARE = PIECE // N_WAVE


STEPS = ((1, 0), (0, -1), (-1, 0), (0, 1))


def signed(d):
    return (d + SIDE // 2 - 1) % SIDE - SIDE // 2 + 1


def reach(offset):
    return sum(abs(signed(d)) for d in offset)


def turned(offset):
    return offset[1], (-offset[0]) % SIDE


def before(offset, step):
    return (offset[0] - step[0]) % SIDE, (offset[1] - step[1]) % SIDE


def plan():
    half = SIDE // 2
    last = [(half, half), (0, half), (half, 0), (0, 0)]
    groups, seen = [], set(last)
    offsets = [(dz, dy) for dz in range(SIDE) for dy in range(SIDE)]
    for offset in sorted(offsets, key=lambda o: (-reach(o), o)):
        if offset in seen:
            continue
        dz, dy = signed(offset[0]), signed(offset[1])
        along = (1 if dz > 0 else -1, 0) if abs(dz) >= abs(dy) else (0, 1 if dy > 0 else -1)
        group = [None] * 4
        for n in range(4):
            group[(STEPS.index(along) + n) % 4] = offset
            seen.add(offset)
            offset = turned(offset)
        groups.append(group)
    return groups + [last]


GROUPS = plan()
PER_CHUNK = len(GROUPS) // CHUNKS
SLOTS = []
for c in range(CHUNKS):
    for d, step in enumerate(STEPS):
        for group in GROUPS[c * PER_CHUNK : (c + 1) * PER_CHUNK]:
            owner = group[d]
            SLOTS.append((owner, before(owner, step) if owner != (0, 0) else owner))


SEND = sorted(
    range(N_BIN), key=lambda k: (-reach(SLOTS[k][1]), k // PER, k % PER_CHUNK, k % PER // PER_CHUNK)
)
PLANE = [owner for owner, _ in SLOTS if owner != (0, 0)]


def iota(shape, dim):
    return lax.broadcasted_iota(jnp.int32, shape, dim)


def nt(a, b):
    return lax.dot_general(a, b, (((1,), (1,)), ((), ())), preferred_element_type=F32)


def mm(a, b):
    return jnp.dot(a, b, preferred_element_type=F32)


def as_row(ref, dtype=jnp.int32):
    v = ref[...].astype(dtype)
    return jnp.concatenate([v[i : i + 1, :] for i in range(v.shape[0])], axis=1)


def kernel(
    src_hbm, den_hbm, bins_hbm, ray_hbm, tab_hbm, out_any,
    src_ref, den_ref, bins_ref, ray_ref, tab_ref, out_ref, load_sem,
    send, esend, recv, erecv, acc, sbuf, crecv, xsend, xrecv, ysend, yrecv, asend, arecv,
    near, t_ssem, t_rsem, met, s_sem, e_ssem, r_sem, e_rsem, c_ssem, c_rsem, x_ssem, x_rsem, y_ssem, y_rsem, a_ssem, a_rsem,
):
    me = lax.axis_index("bin")
    wave = lax.axis_index("wave")
    mz, my = me // SIDE, me & (SIDE - 1)
    mx, core = wave // 2, wave & 1

    def peer(offset):
        return ((mz + offset[0]) & (SIDE - 1)) * SIDE + ((my + offset[1]) & (SIDE - 1))

    loads = [
        pltpu.make_async_copy(given, held, load_sem.at[n])
        for n, (given, held) in enumerate((
            (bins_hbm, bins_ref), (den_hbm, den_ref), (ray_hbm, ray_ref), (src_hbm, src_ref),
            (tab_hbm.at[0], tab_ref),
        ))
    ]
    for load in loads:
        load.start()
    barrier = pltpu.get_barrier_semaphore()

    def greet(bin_at, wave_at):
        pl.semaphore_signal(barrier, inc=1, device_id=(bin_at, wave_at), device_id_type=MESH)

    first_core = mx * 2
    for offset in sorted(PLANE, key=lambda o: -reach(o)):
        greet(peer(offset), first_core)
    for i in range(1, N_X):
        greet(me, ((mx + i) & (N_X - 1)) * 2)
    for step in STEPS:
        greet(peer(step), first_core + 1)
    greet(me, first_core + 1 - core)

    def table_copy(d):
        back = (-STEPS[d][0], -STEPS[d][1])
        return pltpu.make_async_remote_copy(
            src_ref=tab_ref, dst_ref=near.at[d], send_sem=t_ssem.at[d], recv_sem=t_rsem.at[d],
            device_id=(peer(back), wave), device_id_type=MESH,
        )

    def ship():
        for k in SEND:
            owner, host = SLOTS[k]
            own, to = peer(owner), peer(host)
            for out, into, s, r in ((esend, erecv, e_ssem, e_rsem), (send, recv, s_sem, r_sem)):
                if host == (0, 0):
                    pltpu.make_async_copy(out.at[own], into.at[k], r.at[k // PER]).start()
                else:
                    pltpu.make_async_remote_copy(
                        src_ref=out.at[own], dst_ref=into.at[k], send_sem=s,
                        recv_sem=r.at[k // PER], device_id=(to, wave), device_id_type=MESH,
                    ).start()

    @pl.when(core == 1)
    def _():
        pl.semaphore_wait(barrier, 2 * len(STEPS) + 1)
        pl.semaphore_signal(met.at[0], inc=1, device_id=(me, first_core), device_id_type=MESH)

    @pl.when(core == 0)
    def _():
        pl.semaphore_wait(met.at[0], 1)

    loads[4].wait()
    for d in range(4):
        table_copy(d).start()

    for load in loads[:3]:
        load.wait()
    bins = as_row(bins_ref)
    den = as_row(den_ref, F32)
    ray = as_row(ray_ref)
    code = (ray >> 8) * PIECE + ((ray & 15) >> 1) * SHARE + ((ray >> 4) & 15) * 2 + (ray & 1)
    high = (code >> 5).astype(F32)
    low = (code & 31).astype(F32)
    member = jnp.where(iota((N_BIN, CELLS), 0) == bins, 1.0, 0.0)
    upper = jnp.where(iota((CELLS, CELLS), 0) <= iota((CELLS, CELLS), 1), 1.0, 0.0).astype(BF16)
    rank = mm(member.astype(BF16), upper)
    pos = (jnp.sum(rank * member, axis=0, keepdims=True) - 1.0).astype(jnp.int32)
    slot = bins * CAP + pos
    lane = iota((128, CELLS), 0)
    extras = jnp.zeros((N_BIN, 128), F32)
    for k, value in enumerate((den, high, low)):
        place = jnp.where(lane == pos + k * CAP, 1.0, 0.0).astype(BF16)
        extras = extras + nt((member * value).astype(BF16), place)
    for b in range(N_BIN):
        esend[b] = extras[b : b + 1, :]
    loads[3].wait()

    def pack(c):
        hot = jnp.where(iota((ROWS, CELLS), 0) + c * ROWS == slot, 1.0, 0.0).astype(BF16)
        packed = mm(hot, src_ref[...]).astype(BF16)
        send[pl.ds(c * PER, PER)] = packed.reshape(PER, CAP, LEVELS)

    @pl.loop(0, CHUNKS)
    def _(c):
        pack(c)

    @pl.when(core == 0)
    def _():
        pl.semaphore_wait(barrier, 2 * (N_BIN - 1) + 2 * (N_X - 1) + 1)
        pl.semaphore_signal(met.at[1], inc=1, device_id=(me, first_core + 1), device_id_type=MESH)

    @pl.when(core == 1)
    def _():
        pl.semaphore_wait(met.at[1], 1)

    ship()
    acc[...] = jnp.zeros_like(acc)
    for d in range(4):
        table_copy(d).wait_recv()
    ones = jnp.ones((128, LEVELS), BF16)
    ones8 = jnp.ones((8, 128), BF16)

    quarter = ROWS // 4

    def by_table(rows, last):
        parts = [mm(rows[d * quarter : (d + 1) * quarter], near[d]) for d in range(3)]
        if last:
            parts.append(mm(rows[3 * quarter : ROWS - CAP], near[3]))
            parts.append(mm(rows[ROWS - CAP :], tab_ref[...]))
        else:
            parts.append(mm(rows[3 * quarter :], near[3]))
        return jnp.concatenate(parts, axis=0)

    def chunk(c, last=False):
        block = pl.ds(c * PER, PER)
        pltpu.make_async_copy(erecv.at[block], erecv.at[block], e_rsem.at[c]).wait()
        pltpu.make_async_copy(recv.at[block], recv.at[block], r_sem.at[c]).wait()
        extra = jnp.broadcast_to(erecv[block], (PER, CAP, 128)).reshape(ROWS, 128)
        lanes = iota((ROWS, 128), 1)
        own = iota((ROWS, 128), 0) & (CAP - 1)
        dens = mm(jnp.where(lanes == own, extra, 0.0).astype(BF16), ones)
        coded = jnp.where(
            lanes == own + CAP, extra * 32.0, jnp.where(lanes == own + 2 * CAP, extra, 0.0)
        )
        rays = nt(ones8, coded.astype(BF16))[0:1, :].astype(jnp.int32)
        rows = recv[block].reshape(ROWS, LEVELS)
        wide = rows.astype(F32)
        first = (dens * by_table(rows, last) + wide).astype(BF16)
        pops = (dens * by_table(first, last) + wide).astype(BF16)
        return rays, pops

    @pl.loop(0, CHUNKS - 1)
    def _(c):
        rays, pops = chunk(c)
        hot = jnp.where(iota((RAYS, ROWS), 0) == rays, 1.0, 0.0).astype(BF16)
        acc[...] += mm(hot, pops)

    rays, pops = chunk(CHUNKS - 1, last=True)

    pieces = [((mz >> 1) + k) & (PIECES - 1) for k in (2, 1, 3, 0)]

    def pair_copy(n):
        return pltpu.make_async_remote_copy(
            src_ref=sbuf.at[n], dst_ref=crecv.at[n], send_sem=c_ssem.at[n], recv_sem=c_rsem.at[n],
            device_id=(me, mx * 2 + 1 - core), device_id_type=MESH,
        )

    def x_copy(n, i):
        return pltpu.make_async_remote_copy(
            src_ref=xsend.at[n, i - 1], dst_ref=xrecv.at[n, i - 1], send_sem=x_ssem.at[n, i - 1],
            recv_sem=x_rsem.at[n, i - 1],
            device_id=(me, ((mx + i) & (N_X - 1)) * 2 + core), device_id_type=MESH,
        )

    def share(piece, member_x, member_core):
        at = piece * PIECE + (member_x * 2 + member_core) * SHARE
        return pl.ds(pl.multiple_of(at, SHARE), SHARE)

    def sum_cells(n):
        piece = pieces[n]
        here = pl.ds(pl.multiple_of(piece * PIECE, PIECE), PIECE)
        hot = jnp.where(iota((PIECE, ROWS), 0) + piece * PIECE == rays, 1.0, 0.0).astype(BF16)
        acc[here, :] += mm(hot, pops)
        for x in range(N_X):
            sbuf[n, x] = acc[share(piece, x, 1 - core), :].astype(BF16)
        pair_copy(n).start()

    def sum_pair(n):
        pair_copy(n).wait_recv()
        for i in (2, 1, 3):
            x = (mx + i) & (N_X - 1)
            both = acc[share(pieces[n], x, core), :] + crecv[n, x].astype(F32)
            xsend[n, i - 1] = both.astype(BF16)
            x_copy(n, i).start()

    def sum_x(n):
        piece = pieces[n]
        total = acc[share(piece, mx, core), :] + crecv[n, mx].astype(F32)
        for i in (1, 3, 2):
            x_copy(n, i).wait_recv()
            total = total + xrecv[n, i - 1].astype(F32)
        total = total.astype(BF16)
        for j in range(PIECE_BINS):
            ysend[piece * PIECE_BINS + j] = total[2 * j : 2 * j + 2, :]

        for j in sorted(range(PIECE_BINS), key=lambda j: -abs(signed(j % SIDE))):
            to = piece * PIECE_BINS + ((me + j) & (PIECE_BINS - 1))

            @pl.when(to != me)
            def _(to=to):
                pltpu.make_async_remote_copy(
                    src_ref=ysend.at[to], dst_ref=yrecv.at[me], send_sem=y_ssem, recv_sem=y_rsem,
                    device_id=(to, wave), device_id_type=MESH,
                ).start()

    sum_cells(0)
    sum_cells(1)
    sum_pair(0)
    sum_cells(2)
    sum_pair(1)
    sum_cells(3)
    sum_pair(2)
    sum_pair(3)
    for n in range(PIECES):
        sum_x(n)

    pltpu.make_async_copy(ysend.at[me], yrecv.at[me], y_rsem).start()
    pltpu.make_async_copy(yrecv, yrecv, y_rsem).wait()
    asend[...] = jnp.sum(yrecv[...].astype(F32), axis=0)
    for i in (4, 5, 3, 2, 6, 7, 1):
        pltpu.make_async_remote_copy(
            src_ref=asend, dst_ref=arecv.at[wave], send_sem=a_ssem, recv_sem=a_rsem,
            device_id=(me, (wave + i) & (N_WAVE - 1)), device_id_type=MESH,
        ).start()
    pltpu.make_async_copy(asend, arecv.at[wave], a_rsem).start()

    for d in range(4):
        table_copy(d).wait_send()
    away = pl.ds(0, sum(host != (0, 0) for _, host in SLOTS))
    pltpu.make_async_copy(esend.at[away], esend.at[away], e_ssem).wait()
    pltpu.make_async_copy(send.at[away], send.at[away], s_sem).wait()
    rest = pl.ds(0, N_BIN - 1)
    for n in range(PIECES):
        pair_copy(n).wait_send()
        for i in (1, 2, 3):
            x_copy(n, i).wait_send()
    pltpu.make_async_copy(ysend.at[rest], ysend.at[rest], y_ssem).wait()

    pltpu.make_async_copy(arecv, arecv, a_rsem).wait()
    for w in range(N_WAVE):
        out_any[2 * w : 2 * w + 2, :] = arecv[w]
    others = pl.ds(0, N_WAVE - 1)
    pltpu.make_async_copy(arecv.at[others], arecv.at[others], a_ssem).wait()


def per_device(sources, density, temp_bins, ray_index, rate_tables, line_table):
    hbm = pl.BlockSpec(memory_space=pltpu.HBM)
    dma = pltpu.SemaphoreType.DMA
    whole_rays = pl.pallas_call(
        kernel,
        out_shape=jax.ShapeDtypeStruct((RAYS // N_BIN, LEVELS), F32),
        in_specs=[hbm] * 5,
        out_specs=pl.BlockSpec(memory_space=pltpu.VMEM),
        scratch_shapes=[
            pltpu.VMEM((CELLS, LEVELS), BF16),
            pltpu.VMEM((CELLS // 128, 128), BF16),
            pltpu.VMEM((CELLS // 128, 128), jnp.int32),
            pltpu.VMEM((CELLS // 128, 128), jnp.int32),
            pltpu.VMEM((LEVELS, LEVELS), BF16),
            pltpu.VMEM((RAYS // N_BIN, LEVELS), F32),
            dma((5,)),
            pltpu.VMEM((N_BIN, CAP, LEVELS), BF16),
            pltpu.VMEM((N_BIN, 1, 128), F32),
            pltpu.VMEM((N_BIN, CAP, LEVELS), BF16),
            pltpu.VMEM((N_BIN, 1, 128), F32),
            pltpu.VMEM((RAYS, LEVELS), F32),
            pltpu.VMEM((PIECES, N_X, SHARE, LEVELS), BF16),
            pltpu.VMEM((PIECES, N_X, SHARE, LEVELS), BF16),
            pltpu.VMEM((PIECES, N_X - 1, SHARE, LEVELS), BF16),
            pltpu.VMEM((PIECES, N_X - 1, SHARE, LEVELS), BF16),
            pltpu.VMEM((N_BIN, 2, LEVELS), BF16),
            pltpu.VMEM((N_BIN, 2, LEVELS), BF16),
            pltpu.VMEM((2, LEVELS), F32),
            pltpu.VMEM((N_WAVE, 2, LEVELS), F32),
            pltpu.VMEM((4, LEVELS, LEVELS), BF16),
            dma((4,)), dma((4,)), pltpu.SemaphoreType.REGULAR((2,)),
            dma, dma, dma((CHUNKS,)), dma((CHUNKS,)), dma((PIECES,)), dma((PIECES,)),
            dma((PIECES, N_X - 1)), dma((PIECES, N_X - 1)),
            dma, dma, dma, dma,
        ],
        compiler_params=pltpu.CompilerParams(
            collective_id=0, has_side_effects=True, vmem_limit_bytes=24 * 1024 * 1024
        ),
        name="populations",
    )(*(pltpu.with_memory_space_constraint(a, pltpu.HBM) for a in (
        sources,
        density.reshape(4, 128),
        temp_bins.reshape(4, 128),
        ray_index.reshape(4, 128),
        rate_tables,
    )))
    return jnp.dot(
        whole_rays,
        line_table.astype(F32),
        precision=lax.Precision.HIGHEST,
        preferred_element_type=F32,
    )


def solution(mesh):
    in_specs = (
        P(("bin", "wave"), None),
        P(("bin", "wave")),
        P(("bin", "wave"), None),
        P(("bin", "wave")),
        P("bin", None, None),
        P(None, "wave"),
    )
    return jax.shard_map(
        per_device, mesh=mesh, in_specs=in_specs, out_specs=P("bin", "wave"), check_vma=False
    )
```
